32 devices in a mesh: bond: 8 (over y, x, core), outer: 4 (over z).
Axes of the slice: x: 2, y: 2, z: 4, core: 2. Of those that a mesh axis runs over, the one named last changes fastest.
Arguments:
- upper: bfloat16 [128, 128, 128], P(None, 'bond'), may hold values from -4 to 4
- lower: bfloat16 [128, 128, 8, 128], P(None, 'bond', 'outer'), may hold values from -4 to 4
- isometry: bfloat16 [16384, 128], P(('bond', 'outer')), may hold values from -0.046875 to 0.046875
Outputs:
- coarse: float32 [128, 8, 128], P('bond', 'outer')
The draws below stay inside these ranges and needn't reach their ends.
All inputs are finite; a program needn't handle non-finite values.
Results may differ from the reference program's by a relative error of at most 0.004.
Values may be sent and summed in bfloat16 or wider, within the bound.
A program may use at most 64 MiB of HBM per device.

```python
import jax
import jax.numpy as jnp
from jax import lax

D = 128
LOW = 8


def block_scale(stream_key, extent, split, smallest, high):
    level = 1.0
    for axis_at, blocks in split:
        heights = jax.random.uniform(jax.random.fold_in(jax.random.fold_in(stream_key, 6), axis_at), (blocks,), jnp.float32, smallest / len(split), high / len(split))
        level = level * jnp.repeat(jnp.exp(heights), extent[axis_at] // blocks).reshape((-1,) + (1,) * (len(extent) - 1 - axis_at))
    return level


def bell_draw(stream_key, dims, scale, limit, shards=(), kind=jnp.bfloat16):
    values = scale * jax.random.normal(stream_key, dims, jnp.float32)
    if shards:
        values = values * block_scale(stream_key, dims, shards, -0.22, 0.18)
    return jnp.clip(values, -limit, limit).astype(kind)


def setup_inputs(seed: int = 0) -> dict:
    arg_keys = jax.random.split(jax.random.key(seed), 4)
    upper = bell_draw(arg_keys[0], (D, D, D), 0.3, 4.0, ((1, 8),))
    lower = bell_draw(arg_keys[1], (D, D, LOW, D), 0.3, 4.0, ((1, 8), (2, 4)))
    isometry = bell_draw(arg_keys[2], (D * D, D), (D * D) ** -0.5, 0.046875, ((0, 32),))
    return {"upper": upper, "lower": lower, "isometry": isometry}


def reference(upper, lower, isometry):
    iso_full = isometry.astype(jnp.float32).reshape(D, D, D)

    def member(total, slabs):
        upper_slab, lower_slab = slabs
        joined = jnp.einsum("lr,lkx->rkx", upper_slab.astype(jnp.float32), iso_full).astype(jnp.bfloat16)
        paired = jnp.einsum("rkx,kds->drxs", joined.astype(jnp.float32), lower_slab.astype(jnp.float32)).astype(jnp.bfloat16)
        partial_sum = jnp.einsum("drxs,rsy->xdy", paired.astype(jnp.float32), iso_full)
        return total + partial_sum, None

    start = jnp.zeros((D, LOW, D), jnp.float32)
    result, unused = lax.scan(member, start, (upper, lower))
    return result
```

```python
import functools

import jax
import jax.numpy as jnp
from jax import lax
from jax.experimental import pallas as pl
from jax.experimental.pallas import tpu as pltpu
from jax.sharding import PartitionSpec as P

GROUP = 8
MESH = pl.DeviceIdType.MESH


def flip(index, weight):
    return index + weight * (1 - 2 * ((index // weight) % 2))


def plans(size):
    bits = [1 << b for b in range(1, size.bit_length() - 1)]
    return (bits + [1], bits[::-1] + [1])


def doubled(me, earlier):
    blocks = [me]
    for weight in earlier:
        blocks = blocks + [flip(b, weight) for b in blocks]
    return blocks


def kernel(
    bonds, outers, up_in, low, iso_in, out_ref,
    up, iso, isof, left, joined, acc, reduced,
    up_send, up_recv, iso_send, iso_recv, out_send, out_recv, red_send, red_recv,
):
    me = lax.axis_index("bond")
    my_outer = lax.axis_index("outer")
    chunks = up_in.shape[0]
    width = iso_in.shape[1]
    own = up_in.shape[2]
    per_block = iso_in.shape[0] // width
    kinds = plans(bonds)
    stages = len(kinds[0])

    barrier = pltpu.get_barrier_semaphore()
    for step in range(1, bonds):
        pl.semaphore_signal(barrier, inc=1, device_id=(lax.rem(me + step, bonds), my_outer), device_id_type=MESH)
    for step in range(1, outers):
        pl.semaphore_signal(barrier, inc=1, device_id=(me, lax.rem(my_outer + step, outers)), device_id_type=MESH)
    pl.semaphore_wait(barrier, bonds + outers - 2)

    def slot(b, o):
        return b * outers + o

    def outer_copy(step):
        return pltpu.make_async_remote_copy(
            src_ref=iso_in, dst_ref=iso.at[slot(me, my_outer)],
            send_sem=out_send.at[step], recv_sem=out_recv.at[my_outer],
            device_id=(me, lax.rem(my_outer + step, outers)), device_id_type=MESH,
        )

    def outer_arrival(step):
        source = lax.rem(my_outer + step, outers)
        return pltpu.make_async_remote_copy(
            src_ref=iso_in, dst_ref=iso.at[slot(me, source)],
            send_sem=out_send.at[step], recv_sem=out_recv.at[source],
            device_id=(me, source), device_id_type=MESH,
        )

    def up_copies(c, h, stage):
        order = kinds[h]
        partner = flip(me, order[stage])
        copies = []
        for at, block in enumerate(doubled(me, order[:stage])):
            source = up_in.at[c, h] if at == 0 else up.at[c, h, block]
            copies.append(pltpu.make_async_remote_copy(
                src_ref=source, dst_ref=up.at[c, h, block],
                send_sem=up_send.at[c, h, (1 << stage) - 1 + at], recv_sem=up_recv.at[c, h, block],
                device_id=(partner, my_outer), device_id_type=MESH,
            ))
        return copies

    def up_arrivals(c, h, stage):
        order = kinds[h]
        partner = flip(me, order[stage])
        return [
            pltpu.make_async_remote_copy(
                src_ref=up_in.at[c, h], dst_ref=up.at[c, h, block],
                send_sem=up_send.at[c, h, 0], recv_sem=up_recv.at[c, h, block],
                device_id=(partner, my_outer), device_id_type=MESH,
            )
            for block in doubled(partner, order[:stage])
        ]

    def iso_copies(o, h, stage):
        order = kinds[h]
        partner = flip(me, order[stage])
        return [
            pltpu.make_async_remote_copy(
                src_ref=iso.at[slot(block, o)], dst_ref=iso.at[slot(block, o)],
                send_sem=iso_send.at[o, (1 << stage) - 1 + at], recv_sem=iso_recv.at[o, block],
                device_id=(partner, my_outer), device_id_type=MESH,
            )
            for at, block in enumerate(doubled(me, order[:stage]))
        ]

    def iso_arrivals(o, h, stage):
        order = kinds[h]
        partner = flip(me, order[stage])
        return [
            pltpu.make_async_remote_copy(
                src_ref=iso.at[slot(block, o)], dst_ref=iso.at[slot(block, o)],
                send_sem=iso_send.at[o, 0], recv_sem=iso_recv.at[o, block],
                device_id=(partner, my_outer), device_id_type=MESH,
            )
            for block in doubled(partner, order[:stage])
        ]

    def start(copies):
        for copy in copies:
            copy.start()

    def arrive(copies):
        for copy in copies:
            copy.wait_recv()

    for step in range(1, outers):
        outer_copy(step).start()

    @pl.loop(0, chunks)
    def _(c):
        for h in range(2):
            start(up_copies(c, h, 0))

    iso[slot(me, my_outer)] = iso_in[...]

    @pl.loop(0, chunks)
    def _(c):
        for h in range(2):
            up[c, h, me] = up_in[c, h]

    for step in range(outers):
        o = lax.rem(my_outer + step, outers)
        if step:
            outer_arrival(step).wait_recv()
        start(iso_copies(o, step % 2, 0))
    for stage in range(1, stages):
        for step in range(outers):
            o = lax.rem(my_outer + step, outers)
            arrive(iso_arrivals(o, step % 2, stage - 1))
            start(iso_copies(o, step % 2, stage))

    for stage in range(1, stages - 1):
        @pl.loop(0, chunks)
        def _(c):
            for h in range(2):
                arrive(up_arrivals(c, h, stage - 1))
                start(up_copies(c, h, stage))

    def hand_over(c):
        for h in range(2):
            arrive(up_arrivals(c, h, stages - 2))
            start(up_copies(c, h, stages - 1))

    for step in range(outers):
        o = lax.rem(my_outer + step, outers)
        arrive(iso_arrivals(o, step % 2, stages - 1))

    first = pl.multiple_of(me * own, own)

    @pl.loop(0, bonds * outers)
    def _(q):
        for i in range(per_block):
            isof[pl.ds((q * per_block + i) * own, own), :] = iso[
                q, pl.ds(i * width + first, own), :
            ].astype(jnp.float32)

    @pl.loop(0, own)
    def _(k):
        left[pl.ds(k * width, width), :] = isof[pl.ds(k, width, stride=own), :].T.astype(jnp.bfloat16)

    acc[...] = jnp.zeros_like(acc)
    lowers = acc.shape[0]
    hand_over(0)

    @pl.loop(0, chunks)
    def _(c):
        @pl.when(c + 1 < chunks)
        def _():
            hand_over(c + 1)

        for h in range(2):
            arrive(up_arrivals(c, h, stages - 1))

        @pl.loop(0, 2)
        def _(h):
            for pair in range(GROUP // 2):
                w = up[c, h, :, :, pl.ds(pair * 2 * width, 2 * width)].reshape(width, 2 * width)
                j = jnp.dot(left[...], w, preferred_element_type=jnp.float32).astype(jnp.bfloat16)
                for rr in range(2):
                    for k in range(own):
                        joined[pl.ds((pair * 2 + rr) * width, width), pl.ds(k * width, width)] = j[
                            k * width:(k + 1) * width, rr * width:(rr + 1) * width
                        ]
            q = jnp.dot(joined[...], low[...], preferred_element_type=jnp.float32).astype(jnp.bfloat16)
            take = GROUP // per_block
            rows = iso[pl.ds((c * 2 + h) * take, take)].reshape(GROUP * width, width)
            for d in range(lowers):
                lhs = jnp.concatenate(
                    [q[rr * width:(rr + 1) * width, d * width:(d + 1) * width] for rr in range(GROUP)], axis=1
                )
                acc[d] += jnp.dot(lhs, rows, preferred_element_type=jnp.float32).reshape(acc.shape[1:])

    def red_copy(step):
        target = lax.rem(me + step, bonds)
        return pltpu.make_async_remote_copy(
            src_ref=acc.at[:, target], dst_ref=reduced.at[step - 1],
            send_sem=red_send.at[step], recv_sem=red_recv.at[step],
            device_id=(target, my_outer), device_id_type=MESH,
        )

    for step in range(1, bonds):
        red_copy(step).start()
    total = acc[:, me]
    for step in range(1, bonds):
        red_copy(step).wait_recv()
        total = total + reduced[step - 1]
    out_ref[...] = total
    for step in range(1, bonds):
        red_copy(step).wait_send()
    for step in range(1, outers):
        outer_copy(step).wait_send()
    for stage in range(stages):
        for step in range(outers):
            o = lax.rem(my_outer + step, outers)
            for copy in iso_copies(o, step % 2, stage):
                copy.wait_send()

    @pl.loop(0, chunks)
    def _(c):
        for h in range(2):
            for stage in range(stages):
                for copy in up_copies(c, h, stage):
                    copy.wait_send()


def fused(upper, lower, isometry):
    bonds, outers = lax.axis_size("bond"), lax.axis_size("outer")
    width = isometry.shape[1]
    own, lowers = upper.shape[1], lower.shape[2]
    chunks = width // (2 * GROUP)
    up_in = upper.transpose(1, 2, 0).reshape(own, chunks, 2, GROUP * width).transpose(1, 2, 0, 3)
    low = lower.transpose(1, 0, 2, 3).reshape(own * width, lowers * width)
    bf, f32, dma = jnp.bfloat16, jnp.float32, pltpu.SemaphoreType.DMA
    out = pl.pallas_call(
        functools.partial(kernel, bonds, outers),
        out_shape=jax.ShapeDtypeStruct((lowers, own, width), f32),
        in_specs=[pl.BlockSpec(memory_space=pltpu.VMEM)] * 3,
        out_specs=pl.BlockSpec(memory_space=pltpu.VMEM),
        scratch_shapes=[
            pltpu.VMEM((chunks, 2, bonds, own, GROUP * width), bf),
            pltpu.VMEM((bonds * outers, isometry.shape[0], width), bf),
            pltpu.VMEM((width * own, width), f32),
            pltpu.VMEM((own * width, width), bf),
            pltpu.VMEM((GROUP * width, own * width), bf),
            pltpu.VMEM((lowers, bonds, own, width), f32),
            pltpu.VMEM((bonds - 1, lowers, own, width), f32),
            dma((chunks, 2, bonds - 1)),
            dma((chunks, 2, bonds)),
            dma((outers, bonds - 1)),
            dma((outers, bonds)),
            dma((outers,)),
            dma((outers,)),
            dma((bonds,)),
            dma((bonds,)),
        ],
        compiler_params=pltpu.CompilerParams(
            collective_id=0, has_side_effects=True, vmem_limit_bytes=60 * 1024 * 1024
        ),
    )(up_in, low, isometry)
    return out.transpose(1, 0, 2)


def plain(upper, lower, isometry):
    width = isometry.shape[1]
    own = upper.shape[1]
    iso = lax.all_gather(isometry, ("bond", "outer"), axis=0, tiled=True).reshape(width, width, width)
    whole = lax.all_gather(upper, "bond", axis=1, tiled=True)
    mine = lax.dynamic_slice_in_dim(iso, lax.axis_index("bond") * own, own, 1)

    def column(total, item):
        slab, rows = item
        joined = jnp.einsum("ml,lkx->xkm", slab, mine, preferred_element_type=jnp.float32).astype(jnp.bfloat16)
        paired = jnp.einsum("xkm,mkds->xds", joined, lower, preferred_element_type=jnp.float32).astype(jnp.bfloat16)
        return total + jnp.einsum("xds,sy->xdy", paired, rows, preferred_element_type=jnp.float32), None

    start_total = jnp.zeros((width, lower.shape[2], width), jnp.float32)
    total, _ = lax.scan(column, start_total, (whole.transpose(2, 0, 1), iso))
    return lax.psum_scatter(total, "bond", scatter_dimension=0, tiled=True)


def on_device(upper, lower, isometry):
    bonds = lax.axis_size("bond")
    width = isometry.shape[1]
    rows = isometry.shape[0] // width
    fits = (
        upper.shape[1] % 16 == 0 and bonds >= 4 and bonds & (bonds - 1) == 0
        and width % (2 * GROUP) == 0 and rows > 0 and GROUP % rows == 0
    )
    return (fused if fits else plain)(upper, lower, isometry)


def solution(mesh):
    return jax.shard_map(
        on_device,
        mesh=mesh,
        in_specs=(
            P(None, "bond", None),
            P(None, "bond", "outer", None),
            P(("bond", "outer"), None),
        ),
        out_specs=P("bond", "outer", None),
        check_vma=False,
    )
```

```python
import functools

import jax
import jax.numpy as jnp
from jax import lax
from jax.experimental import pallas as pl
from jax.experimental.pallas import tpu as pltpu
from jax.sharding import PartitionSpec as P

GROUP = 8
MESH = pl.DeviceIdType.MESH


def flip(index, weight):
    return index + weight * (1 - 2 * ((index // weight) % 2))


def plans(size):
    bits = [1 << b for b in range(1, size.bit_length() - 1)]
    return (bits + [1], bits[::-1] + [1])


def doubled(me, earlier):
    blocks = [me]
    for weight in earlier:
        blocks = blocks + [flip(b, weight) for b in blocks]
    return blocks


def kernel(
    bonds, outers, up_in, low, iso_in, out_ref,
    up, iso, thin, isof, left, joined, pairs, acc, reduced,
    thin_send, thin_recv, up_send, up_recv, iso_send, iso_recv, out_send, out_recv, red_send, red_recv,
):
    me = lax.axis_index("bond")
    my_outer = lax.axis_index("outer")
    chunks = up_in.shape[0] // 2
    per_block, width = iso_in.shape[:2]
    own = up_in.shape[2]
    lowers = low.shape[0]
    kinds = plans(bonds)
    stages = len(kinds[0])

    barrier = pltpu.get_barrier_semaphore()
    peers = [
        (lax.rem(me + i, bonds), lax.rem(my_outer + j, outers))
        for i in range(bonds) for j in range(outers) if i or j
    ]
    for peer in peers:
        pl.semaphore_signal(barrier, inc=1, device_id=peer, device_id_type=MESH)
    pl.semaphore_wait(barrier, len(peers))

    def slot(b, o):
        return b * outers + o

    def thin_copy(at):
        b, o = peers[at]
        return pltpu.make_async_remote_copy(
            src_ref=iso_in.at[:, pl.ds(pl.multiple_of(b * own, own), own)],
            dst_ref=thin.at[slot(me, my_outer)],
            send_sem=thin_send.at[at], recv_sem=thin_recv.at[slot(me, my_outer)],
            device_id=(b, o), device_id_type=MESH,
        )

    def thin_arrival(at):
        b, o = peers[at]
        return pltpu.make_async_remote_copy(
            src_ref=thin.at[slot(b, o)], dst_ref=thin.at[slot(b, o)],
            send_sem=thin_send.at[at], recv_sem=thin_recv.at[slot(b, o)],
            device_id=(b, o), device_id_type=MESH,
        )

    def outer_copy(step):
        return pltpu.make_async_remote_copy(
            src_ref=iso_in, dst_ref=iso.at[slot(me, my_outer)],
            send_sem=out_send.at[step], recv_sem=out_recv.at[my_outer],
            device_id=(me, lax.rem(my_outer + step, outers)), device_id_type=MESH,
        )

    def outer_arrival(step):
        source = lax.rem(my_outer + step, outers)
        return pltpu.make_async_remote_copy(
            src_ref=iso_in, dst_ref=iso.at[slot(me, source)],
            send_sem=out_send.at[step], recv_sem=out_recv.at[source],
            device_id=(me, source), device_id_type=MESH,
        )

    def up_copies(c, h, stage):
        order = kinds[h]
        partner = flip(me, order[stage])
        copies = []
        for at, block in enumerate(doubled(me, order[:stage])):
            source = up_in.at[c * 2 + h] if at == 0 else up.at[c * 2 + h, block]
            copies.append(pltpu.make_async_remote_copy(
                src_ref=source, dst_ref=up.at[c * 2 + h, block],
                send_sem=up_send.at[c, h, (1 << stage) - 1 + at], recv_sem=up_recv.at[c, h, block],
                device_id=(partner, my_outer), device_id_type=MESH,
            ))
        return copies

    def up_arrivals(c, h, stage):
        order = kinds[h]
        partner = flip(me, order[stage])
        return [
            pltpu.make_async_remote_copy(
                src_ref=up_in.at[c * 2 + h], dst_ref=up.at[c * 2 + h, block],
                send_sem=up_send.at[c, h, 0], recv_sem=up_recv.at[c, h, block],
                device_id=(partner, my_outer), device_id_type=MESH,
            )
            for block in doubled(partner, order[:stage])
        ]

    def iso_copies(o, h, stage):
        order = kinds[h]
        partner = flip(me, order[stage])
        return [
            pltpu.make_async_remote_copy(
                src_ref=iso.at[slot(block, o)], dst_ref=iso.at[slot(block, o)],
                send_sem=iso_send.at[o, (1 << stage) - 1 + at], recv_sem=iso_recv.at[o, block],
                device_id=(partner, my_outer), device_id_type=MESH,
            )
            for at, block in enumerate(doubled(me, order[:stage]))
        ]

    def iso_arrivals(o, h, stage):
        order = kinds[h]
        partner = flip(me, order[stage])
        return [
            pltpu.make_async_remote_copy(
                src_ref=iso.at[slot(block, o)], dst_ref=iso.at[slot(block, o)],
                send_sem=iso_send.at[o, 0], recv_sem=iso_recv.at[o, block],
                device_id=(partner, my_outer), device_id_type=MESH,
            )
            for block in doubled(partner, order[:stage])
        ]

    def start(copies):
        for copy in copies:
            copy.start()

    def arrive(copies):
        for copy in copies:
            copy.wait_recv()

    for at in range(len(peers)):
        thin_copy(at).start()
    for step in range(1, outers):
        outer_copy(step).start()

    @pl.loop(0, chunks)
    def _(c):
        for h in range(2):
            start(up_copies(c, h, 0))

    first = pl.multiple_of(me * own, own)
    iso[slot(me, my_outer)] = iso_in[...]
    thin[slot(me, my_outer)] = iso_in[:, pl.ds(first, own)]

    @pl.loop(0, 2 * chunks)
    def _(g):
        up[g, me] = up_in[g]

    acc[...] = jnp.zeros_like(acc)

    for stage in range(1, stages - 1):
        @pl.loop(0, chunks)
        def _(c):
            for h in range(2):
                arrive(up_arrivals(c, h, stage - 1))
                start(up_copies(c, h, stage))

    def hand_over(c):
        for h in range(2):
            arrive(up_arrivals(c, h, stages - 2))
            start(up_copies(c, h, stages - 1))

    def iso_stage(stage):
        for step in range(outers):
            o = lax.rem(my_outer + step, outers)
            if stage:
                arrive(iso_arrivals(o, step % 2, stage - 1))
            elif step:
                outer_arrival(step).wait_recv()
            if stage < stages:
                start(iso_copies(o, step % 2, stage))

    for at in range(len(peers)):
        thin_arrival(at).wait_recv()
    hand_over(0)

    @pl.loop(0, bonds * outers)
    def _(q):
        for i in range(per_block):
            isof[pl.ds((q * per_block + i) * own, own), :] = thin[q, i].astype(jnp.float32)

    @pl.loop(0, own)
    def _(k):
        left[pl.ds(k * width, width), :] = isof[pl.ds(k, width, stride=own), :].T.astype(jnp.bfloat16)

    pace = max(1, (chunks - 1) // stages)

    @pl.loop(0, chunks)
    def _(c):
        @pl.when(c + 1 < chunks)
        def _():
            hand_over(c + 1)

        for stage in range(stages):
            @pl.when(c == min(chunks - 1, 1 + stage * pace))
            def _():
                iso_stage(stage)

        for h in range(2):
            arrive(up_arrivals(c, h, stages - 1))

        @pl.loop(0, 2)
        def _(h):
            g = c * 2 + h
            for pair in range(GROUP // 2):
                w = jnp.concatenate(
                    [up[g, :, 2 * pair + rr].reshape(width, width) for rr in range(2)], axis=1
                )
                j = jnp.dot(left[...], w, preferred_element_type=jnp.float32).astype(jnp.bfloat16)
                for rr in range(2):
                    for k in range(own):
                        joined[pl.ds((pair * 2 + rr) * width, width), pl.ds(k * width, width)] = j[
                            k * width:(k + 1) * width, rr * width:(rr + 1) * width
                        ]
            right = jnp.concatenate([low[d] for d in range(lowers)], axis=1)
            pairs[g] = jnp.dot(joined[...], right, preferred_element_type=jnp.float32).astype(jnp.bfloat16)

    iso_stage(stages)
    take = GROUP // per_block

    @pl.loop(0, 2 * chunks)
    def _(g):
        rows = iso[pl.ds(g * take, take)].reshape(GROUP * width, width)
        lhs = jnp.concatenate([
            jnp.concatenate([
                pairs[g, pl.ds(rr * width, width), pl.ds(d * width, width)] for rr in range(GROUP)
            ], axis=1) for d in range(lowers)
        ], axis=0)
        acc[...] += jnp.dot(lhs, rows, preferred_element_type=jnp.float32).reshape(acc.shape)

    def red_copy(step):
        target = lax.rem(me + step, bonds)
        return pltpu.make_async_remote_copy(
            src_ref=acc.at[:, target], dst_ref=reduced.at[step - 1],
            send_sem=red_send.at[step], recv_sem=red_recv.at[step],
            device_id=(target, my_outer), device_id_type=MESH,
        )

    for step in range(1, bonds):
        red_copy(step).start()
    total = acc[:, me]
    for step in range(1, bonds):
        red_copy(step).wait_recv()
        total = total + reduced[step - 1]
    out_ref[...] = total
    for step in range(1, bonds):
        red_copy(step).wait_send()
    for at in range(len(peers)):
        thin_copy(at).wait_send()
    for step in range(1, outers):
        outer_copy(step).wait_send()
    for stage in range(stages):
        for step in range(outers):
            o = lax.rem(my_outer + step, outers)
            for copy in iso_copies(o, step % 2, stage):
                copy.wait_send()

    @pl.loop(0, chunks)
    def _(c):
        for h in range(2):
            for stage in range(stages):
                for copy in up_copies(c, h, stage):
                    copy.wait_send()


def fused(upper, lower, isometry):
    bonds, outers = lax.axis_size("bond"), lax.axis_size("outer")
    width = isometry.shape[1]
    own, lowers = upper.shape[1], lower.shape[2]
    groups = width // GROUP
    up_in = upper.transpose(2, 1, 0).reshape(groups, GROUP, own, width)
    low = lower.transpose(2, 1, 0, 3).reshape(lowers, own * width, width)
    iso_in = isometry.reshape(-1, width, width)
    bf, f32, dma = jnp.bfloat16, jnp.float32, pltpu.SemaphoreType.DMA
    out = pl.pallas_call(
        functools.partial(kernel, bonds, outers),
        out_shape=jax.ShapeDtypeStruct((lowers, own, width), f32),
        in_specs=[pl.BlockSpec(memory_space=pltpu.VMEM)] * 3,
        out_specs=pl.BlockSpec(memory_space=pltpu.VMEM),
        scratch_shapes=[
            pltpu.VMEM((groups, bonds, GROUP, own, width), bf),
            pltpu.VMEM((bonds * outers, *iso_in.shape), bf),
            pltpu.VMEM((bonds * outers, iso_in.shape[0], own, width), bf),
            pltpu.VMEM((width * own, width), f32),
            pltpu.VMEM((own * width, width), bf),
            pltpu.VMEM((GROUP * width, own * width), bf),
            pltpu.VMEM((groups, GROUP * width, lowers * width), bf),
            pltpu.VMEM((lowers, bonds, own, width), f32),
            pltpu.VMEM((bonds - 1, lowers, own, width), f32),
            dma((bonds * outers - 1,)),
            dma((bonds * outers,)),
            dma((groups // 2, 2, bonds - 1)),
            dma((groups // 2, 2, bonds)),
            dma((outers, bonds - 1)),
            dma((outers, bonds)),
            dma((outers,)),
            dma((outers,)),
            dma((bonds,)),
            dma((bonds,)),
        ],
        compiler_params=pltpu.CompilerParams(
            collective_id=0, has_side_effects=True, vmem_limit_bytes=60 * 1024 * 1024
        ),
    )(up_in, low, iso_in)
    return out.transpose(1, 0, 2)


def plain(upper, lower, isometry):
    width = isometry.shape[1]
    own = upper.shape[1]
    iso = lax.all_gather(isometry, ("bond", "outer"), axis=0, tiled=True).reshape(width, width, width)
    whole = lax.all_gather(upper, "bond", axis=1, tiled=True)
    mine = lax.dynamic_slice_in_dim(iso, lax.axis_index("bond") * own, own, 1)

    def column(total, item):
        slab, rows = item
        joined = jnp.einsum("ml,lkx->xkm", slab, mine, preferred_element_type=jnp.float32).astype(jnp.bfloat16)
        paired = jnp.einsum("xkm,mkds->xds", joined, lower, preferred_element_type=jnp.float32).astype(jnp.bfloat16)
        return total + jnp.einsum("xds,sy->xdy", paired, rows, preferred_element_type=jnp.float32), None

    start_total = jnp.zeros((width, lower.shape[2], width), jnp.float32)
    total, _ = lax.scan(column, start_total, (whole.transpose(2, 0, 1), iso))
    return lax.psum_scatter(total, "bond", scatter_dimension=0, tiled=True)


def on_device(upper, lower, isometry):
    bonds = lax.axis_size("bond")
    width = isometry.shape[1]
    rows = isometry.shape[0] // width
    fits = (
        upper.shape[1] % 16 == 0 and bonds >= 4 and bonds & (bonds - 1) == 0
        and width % (2 * GROUP) == 0 and rows > 0 and GROUP % rows == 0
    )
    return (fused if fits else plain)(upper, lower, isometry)


def solution(mesh):
    return jax.shard_map(
        on_device,
        mesh=mesh,
        in_specs=(
            P(None, "bond", None),
            P(None, "bond", "outer", None),
            P(("bond", "outer"), None),
        ),
        out_specs=P("bond", "outer", None),
        check_vma=False,
    )
```

```python
import functools

import jax
import jax.numpy as jnp
from jax import lax
from jax.experimental import pallas as pl
from jax.experimental.pallas import tpu as pltpu
from jax.sharding import PartitionSpec as P

GROUP = 8
MESH = pl.DeviceIdType.MESH


def flip(index, weight):
    return index + weight * (1 - 2 * ((index // weight) % 2))


def plans(size):
    bits = [1 << b for b in range(1, size.bit_length() - 1)]
    return (bits + [1], bits[::-1] + [1])


def doubled(me, earlier):
    blocks = [me]
    for weight in earlier:
        blocks = blocks + [flip(b, weight) for b in blocks]
    return blocks


def kernel(
    bonds, outers, up_in, low, iso_in, out_ref,
    up, iso, thin, isof, left, joined, pairs, acc, reduced,
    thin_send, thin_recv, up_send, up_recv, iso_send, iso_recv, out_send, out_recv, red_send, red_recv,
):
    me = lax.axis_index("bond")
    my_outer = lax.axis_index("outer")
    chunks = up_in.shape[0] // 2
    per_block, width = iso_in.shape[:2]
    own = up_in.shape[2]
    lowers = low.shape[0]
    kinds = plans(bonds)
    stages = len(kinds[0])

    barrier = pltpu.get_barrier_semaphore()
    peers = [
        (lax.rem(me + i, bonds), lax.rem(my_outer + j, outers))
        for i in range(bonds) for j in range(outers) if i or j
    ]
    for peer in peers:
        pl.semaphore_signal(barrier, inc=1, device_id=peer, device_id_type=MESH)
    pl.semaphore_wait(barrier, len(peers))

    def slot(b, o):
        return b * outers + o

    def thin_copy(at):
        b, o = peers[at]
        return pltpu.make_async_remote_copy(
            src_ref=iso_in.at[:, pl.ds(pl.multiple_of(b * own, own), own)],
            dst_ref=thin.at[slot(me, my_outer)],
            send_sem=thin_send.at[at], recv_sem=thin_recv.at[slot(me, my_outer)],
            device_id=(b, o), device_id_type=MESH,
        )

    def thin_arrival(at):
        b, o = peers[at]
        return pltpu.make_async_remote_copy(
            src_ref=thin.at[slot(b, o)], dst_ref=thin.at[slot(b, o)],
            send_sem=thin_send.at[at], recv_sem=thin_recv.at[slot(b, o)],
            device_id=(b, o), device_id_type=MESH,
        )

    def outer_copy(step):
        return pltpu.make_async_remote_copy(
            src_ref=iso_in, dst_ref=iso.at[slot(me, my_outer)],
            send_sem=out_send.at[step], recv_sem=out_recv.at[my_outer],
            device_id=(me, lax.rem(my_outer + step, outers)), device_id_type=MESH,
        )

    def outer_arrival(step):
        source = lax.rem(my_outer + step, outers)
        return pltpu.make_async_remote_copy(
            src_ref=iso_in, dst_ref=iso.at[slot(me, source)],
            send_sem=out_send.at[step], recv_sem=out_recv.at[source],
            device_id=(me, source), device_id_type=MESH,
        )

    def up_copies(c, h, stage):
        order = kinds[h]
        partner = flip(me, order[stage])
        copies = []
        for at, block in enumerate(doubled(me, order[:stage])):
            source = up_in.at[c * 2 + h] if at == 0 else up.at[c * 2 + h, block]
            copies.append(pltpu.make_async_remote_copy(
                src_ref=source, dst_ref=up.at[c * 2 + h, block],
                send_sem=up_send.at[c, h, (1 << stage) - 1 + at], recv_sem=up_recv.at[c, h, block],
                device_id=(partner, my_outer), device_id_type=MESH,
            ))
        return copies

    def up_arrivals(c, h, stage):
        order = kinds[h]
        partner = flip(me, order[stage])
        return [
            pltpu.make_async_remote_copy(
                src_ref=up_in.at[c * 2 + h], dst_ref=up.at[c * 2 + h, block],
                send_sem=up_send.at[c, h, 0], recv_sem=up_recv.at[c, h, block],
                device_id=(partner, my_outer), device_id_type=MESH,
            )
            for block in doubled(partner, order[:stage])
        ]

    def iso_copies(o, h, stage):
        order = kinds[h]
        partner = flip(me, order[stage])
        return [
            pltpu.make_async_remote_copy(
                src_ref=iso.at[slot(block, o)], dst_ref=iso.at[slot(block, o)],
                send_sem=iso_send.at[o, (1 << stage) - 1 + at], recv_sem=iso_recv.at[o, block],
                device_id=(partner, my_outer), device_id_type=MESH,
            )
            for at, block in enumerate(doubled(me, order[:stage]))
        ]

    def iso_arrivals(o, h, stage):
        order = kinds[h]
        partner = flip(me, order[stage])
        return [
            pltpu.make_async_remote_copy(
                src_ref=iso.at[slot(block, o)], dst_ref=iso.at[slot(block, o)],
                send_sem=iso_send.at[o, 0], recv_sem=iso_recv.at[o, block],
                device_id=(partner, my_outer), device_id_type=MESH,
            )
            for block in doubled(partner, order[:stage])
        ]

    def start(copies):
        for copy in copies:
            copy.start()

    def arrive(copies):
        for copy in copies:
            copy.wait_recv()

    for at in range(len(peers)):
        thin_copy(at).start()
    for step in range(1, outers):
        outer_copy(step).start()

    @pl.loop(0, chunks)
    def _(c):
        for h in range(2):
            start(up_copies(c, h, 0))

    first = pl.multiple_of(me * own, own)
    iso[slot(me, my_outer)] = iso_in[...]
    thin[slot(me, my_outer)] = iso_in[:, pl.ds(first, own)]

    @pl.loop(0, 2 * chunks)
    def _(g):
        up[g, me] = up_in[g]

    acc[...] = jnp.zeros_like(acc)

    for stage in range(1, stages - 1):
        @pl.loop(0, chunks)
        def _(c):
            for h in range(2):
                arrive(up_arrivals(c, h, stage - 1))
                start(up_copies(c, h, stage))

    def hand_over(c):
        for h in range(2):
            arrive(up_arrivals(c, h, stages - 2))
            start(up_copies(c, h, stages - 1))

    def iso_stage(stage):
        for step in range(outers):
            o = lax.rem(my_outer + step, outers)
            if stage:
                arrive(iso_arrivals(o, step % 2, stage - 1))
            elif step:
                outer_arrival(step).wait_recv()
            if stage < stages:
                start(iso_copies(o, step % 2, stage))

    for at in range(len(peers)):
        thin_arrival(at).wait_recv()
    hand_over(0)

    @pl.loop(0, bonds * outers)
    def _(q):
        for i in range(per_block):
            isof[pl.ds((q * per_block + i) * own, own), :] = thin[q, i].astype(jnp.float32)

    @pl.loop(0, own)
    def _(k):
        left[pl.ds(k * width, width), :] = isof[pl.ds(k, width, stride=own), :].T.astype(jnp.bfloat16)

    pace = max(1, (chunks - 1) // stages)

    @pl.loop(0, chunks)
    def _(c):
        @pl.when(c + 1 < chunks)
        def _():
            hand_over(c + 1)

        for stage in range(stages):
            @pl.when(c == min(chunks - 1, 1 + stage * pace))
            def _():
                iso_stage(stage)

        for h in range(2):
            arrive(up_arrivals(c, h, stages - 1))

        for pair in range(GROUP):
            h, at = divmod(2 * pair, GROUP)
            w = jnp.concatenate([up[c * 2 + h, :, at + rr].reshape(width, width) for rr in range(2)], axis=1)
            j = jnp.dot(left[...], w, preferred_element_type=jnp.float32).astype(jnp.bfloat16)
            for rr in range(2):
                for k in range(own):
                    joined[h, pl.ds((at + rr) * width, width), pl.ds(k * width, width)] = j[
                        k * width:(k + 1) * width, rr * width:(rr + 1) * width
                    ]
        right = jnp.concatenate([low[d] for d in range(lowers)], axis=1)

        @pl.loop(0, 2)
        def _(h):
            pairs[c * 2 + h] = jnp.dot(joined[h], right, preferred_element_type=jnp.float32).astype(jnp.bfloat16)

    iso_stage(stages)
    take = GROUP // per_block

    @pl.loop(0, 2 * chunks)
    def _(g):
        rows = iso[pl.ds(g * take, take)].reshape(GROUP * width, width)
        lhs = jnp.concatenate([
            jnp.concatenate([
                pairs[g, pl.ds(rr * width, width), pl.ds(d * width, width)] for rr in range(GROUP)
            ], axis=1) for d in range(lowers)
        ], axis=0)
        acc[...] += jnp.dot(lhs, rows, preferred_element_type=jnp.float32).reshape(acc.shape)

    def red_copy(step):
        target = lax.rem(me + step, bonds)
        return pltpu.make_async_remote_copy(
            src_ref=acc.at[:, target], dst_ref=reduced.at[step - 1],
            send_sem=red_send.at[step], recv_sem=red_recv.at[step],
            device_id=(target, my_outer), device_id_type=MESH,
        )

    for step in range(1, bonds):
        red_copy(step).start()
    total = acc[:, me]
    for step in range(1, bonds):
        red_copy(step).wait_recv()
        total = total + reduced[step - 1]
    out_ref[...] = total
    for step in range(1, bonds):
        red_copy(step).wait_send()
    for at in range(len(peers)):
        thin_copy(at).wait_send()
    for step in range(1, outers):
        outer_copy(step).wait_send()
    for stage in range(stages):
        for step in range(outers):
            o = lax.rem(my_outer + step, outers)
            for copy in iso_copies(o, step % 2, stage):
                copy.wait_send()

    @pl.loop(0, chunks)
    def _(c):
        for h in range(2):
            for stage in range(stages):
                for copy in up_copies(c, h, stage):
                    copy.wait_send()


def fused(upper, lower, isometry):
    bonds, outers = lax.axis_size("bond"), lax.axis_size("outer")
    width = isometry.shape[1]
    own, lowers = upper.shape[1], lower.shape[2]
    groups = width // GROUP
    up_in = upper.transpose(2, 1, 0).reshape(groups, GROUP, own, width)
    low = lower.transpose(2, 1, 0, 3).reshape(lowers, own * width, width)
    iso_in = isometry.reshape(-1, width, width)
    bf, f32, dma = jnp.bfloat16, jnp.float32, pltpu.SemaphoreType.DMA
    out = pl.pallas_call(
        functools.partial(kernel, bonds, outers),
        out_shape=jax.ShapeDtypeStruct((lowers, own, width), f32),
        in_specs=[pl.BlockSpec(memory_space=pltpu.VMEM)] * 3,
        out_specs=pl.BlockSpec(memory_space=pltpu.VMEM),
        scratch_shapes=[
            pltpu.VMEM((groups, bonds, GROUP, own, width), bf),
            pltpu.VMEM((bonds * outers, *iso_in.shape), bf),
            pltpu.VMEM((bonds * outers, iso_in.shape[0], own, width), bf),
            pltpu.VMEM((width * own, width), f32),
            pltpu.VMEM((own * width, width), bf),
            pltpu.VMEM((2, GROUP * width, own * width), bf),
            pltpu.VMEM((groups, GROUP * width, lowers * width), bf),
            pltpu.VMEM((lowers, bonds, own, width), f32),
            pltpu.VMEM((bonds - 1, lowers, own, width), f32),
            dma((bonds * outers - 1,)),
            dma((bonds * outers,)),
            dma((groups // 2, 2, bonds - 1)),
            dma((groups // 2, 2, bonds)),
            dma((outers, bonds - 1)),
            dma((outers, bonds)),
            dma((outers,)),
            dma((outers,)),
            dma((bonds,)),
            dma((bonds,)),
        ],
        compiler_params=pltpu.CompilerParams(
            collective_id=0, has_side_effects=True, vmem_limit_bytes=60 * 1024 * 1024
        ),
    )(up_in, low, iso_in)
    return out.transpose(1, 0, 2)


def plain(upper, lower, isometry):
    width = isometry.shape[1]
    own = upper.shape[1]
    iso = lax.all_gather(isometry, ("bond", "outer"), axis=0, tiled=True).reshape(width, width, width)
    whole = lax.all_gather(upper, "bond", axis=1, tiled=True)
    mine = lax.dynamic_slice_in_dim(iso, lax.axis_index("bond") * own, own, 1)

    def column(total, item):
        slab, rows = item
        joined = jnp.einsum("ml,lkx->xkm", slab, mine, preferred_element_type=jnp.float32).astype(jnp.bfloat16)
        paired = jnp.einsum("xkm,mkds->xds", joined, lower, preferred_element_type=jnp.float32).astype(jnp.bfloat16)
        return total + jnp.einsum("xds,sy->xdy", paired, rows, preferred_element_type=jnp.float32), None

    start_total = jnp.zeros((width, lower.shape[2], width), jnp.float32)
    total, _ = lax.scan(column, start_total, (whole.transpose(2, 0, 1), iso))
    return lax.psum_scatter(total, "bond", scatter_dimension=0, tiled=True)


def on_device(upper, lower, isometry):
    bonds = lax.axis_size("bond")
    width = isometry.shape[1]
    rows = isometry.shape[0] // width
    fits = (
        upper.shape[1] % 16 == 0 and bonds >= 4 and bonds & (bonds - 1) == 0
        and width % (2 * GROUP) == 0 and rows > 0 and GROUP % rows == 0
    )
    return (fused if fits else plain)(upper, lower, isometry)


def solution(mesh):
    return jax.shard_map(
        on_device,
        mesh=mesh,
        in_specs=(
            P(None, "bond", None),
            P(None, "bond", "outer", None),
            P(("bond", "outer"), None),
        ),
        out_specs=P("bond", "outer", None),
        check_vma=False,
    )
```

```python
import functools

import jax
import jax.numpy as jnp
from jax import lax
from jax.experimental import pallas as pl
from jax.experimental.pallas import tpu as pltpu
from jax.sharding import PartitionSpec as P

GROUP = 8
MESH = pl.DeviceIdType.MESH


def flip(index, weight):
    return index + weight * (1 - 2 * ((index // weight) % 2))


def plans(size):
    bits = [1 << b for b in range(1, size.bit_length() - 1)]
    return (bits + [1], bits[::-1] + [1])


def doubled(me, earlier):
    blocks = [me]
    for weight in earlier:
        blocks = blocks + [flip(b, weight) for b in blocks]
    return blocks


def kernel(
    bonds, outers, up_in, low, iso_in, out_ref,
    up, iso, thin, isof, left, joined, pairs, acc, reduced,
    thin_send, thin_recv, up_send, up_recv, iso_send, iso_recv, out_send, out_recv, red_send, red_recv,
):
    me = lax.axis_index("bond")
    my_outer = lax.axis_index("outer")
    chunks = up_in.shape[0] // 2
    per_block, width = iso_in.shape[:2]
    own = up_in.shape[2]
    lowers = low.shape[0]
    kinds = plans(bonds)
    stages = len(kinds[0])

    barrier = pltpu.get_barrier_semaphore()
    peers = [
        (lax.rem(me + i, bonds), lax.rem(my_outer + j, outers))
        for i in range(bonds) for j in range(outers) if i or j
    ]
    for peer in peers:
        pl.semaphore_signal(barrier, inc=1, device_id=peer, device_id_type=MESH)
    pl.semaphore_wait(barrier, len(peers))

    def slot(b, o):
        return b * outers + o

    def thin_copy(at):
        b, o = peers[at]
        return pltpu.make_async_remote_copy(
            src_ref=iso_in.at[:, pl.ds(pl.multiple_of(b * own, own), own)],
            dst_ref=thin.at[slot(me, my_outer)],
            send_sem=thin_send.at[at], recv_sem=thin_recv.at[slot(me, my_outer)],
            device_id=(b, o), device_id_type=MESH,
        )

    def thin_arrival(at):
        b, o = peers[at]
        return pltpu.make_async_remote_copy(
            src_ref=thin.at[slot(b, o)], dst_ref=thin.at[slot(b, o)],
            send_sem=thin_send.at[at], recv_sem=thin_recv.at[slot(b, o)],
            device_id=(b, o), device_id_type=MESH,
        )

    def outer_copy(step):
        return pltpu.make_async_remote_copy(
            src_ref=iso_in, dst_ref=iso.at[slot(me, my_outer)],
            send_sem=out_send.at[step], recv_sem=out_recv.at[my_outer],
            device_id=(me, lax.rem(my_outer + step, outers)), device_id_type=MESH,
        )

    def outer_arrival(step):
        source = lax.rem(my_outer + step, outers)
        return pltpu.make_async_remote_copy(
            src_ref=iso_in, dst_ref=iso.at[slot(me, source)],
            send_sem=out_send.at[step], recv_sem=out_recv.at[source],
            device_id=(me, source), device_id_type=MESH,
        )

    def up_copies(c, h, stage):
        order = kinds[h]
        partner = flip(me, order[stage])
        copies = []
        for at, block in enumerate(doubled(me, order[:stage])):
            source = up_in.at[c * 2 + h] if at == 0 else up.at[c * 2 + h, block]
            copies.append(pltpu.make_async_remote_copy(
                src_ref=source, dst_ref=up.at[c * 2 + h, block],
                send_sem=up_send.at[c, h, (1 << stage) - 1 + at], recv_sem=up_recv.at[c, h, block],
                device_id=(partner, my_outer), device_id_type=MESH,
            ))
        return copies

    def up_arrivals(c, h, stage):
        order = kinds[h]
        partner = flip(me, order[stage])
        return [
            pltpu.make_async_remote_copy(
                src_ref=up_in.at[c * 2 + h], dst_ref=up.at[c * 2 + h, block],
                send_sem=up_send.at[c, h, 0], recv_sem=up_recv.at[c, h, block],
                device_id=(partner, my_outer), device_id_type=MESH,
            )
            for block in doubled(partner, order[:stage])
        ]

    def iso_copies(o, h, stage):
        order = kinds[h]
        partner = flip(me, order[stage])
        return [
            pltpu.make_async_remote_copy(
                src_ref=iso.at[slot(block, o)], dst_ref=iso.at[slot(block, o)],
                send_sem=iso_send.at[o, (1 << stage) - 1 + at], recv_sem=iso_recv.at[o, block],
                device_id=(partner, my_outer), device_id_type=MESH,
            )
            for at, block in enumerate(doubled(me, order[:stage]))
        ]

    def iso_arrivals(o, h, stage):
        order = kinds[h]
        partner = flip(me, order[stage])
        return [
            pltpu.make_async_remote_copy(
                src_ref=iso.at[slot(block, o)], dst_ref=iso.at[slot(block, o)],
                send_sem=iso_send.at[o, 0], recv_sem=iso_recv.at[o, block],
                device_id=(partner, my_outer), device_id_type=MESH,
            )
            for block in doubled(partner, order[:stage])
        ]

    def start(copies):
        for copy in copies:
            copy.start()

    def arrive(copies):
        for copy in copies:
            copy.wait_recv()

    for at in range(len(peers)):
        thin_copy(at).start()
    for step in range(1, outers):
        outer_copy(step).start()

    @pl.loop(0, chunks)
    def _(c):
        for h in range(2):
            start(up_copies(c, h, 0))

    first = pl.multiple_of(me * own, own)
    iso[slot(me, my_outer)] = iso_in[...]
    thin[slot(me, my_outer)] = iso_in[:, pl.ds(first, own)]

    @pl.loop(0, 2 * chunks)
    def _(g):
        up[g, me] = up_in[g]

    acc[...] = jnp.zeros_like(acc)

    for stage in range(1, stages - 1):
        @pl.loop(0, chunks)
        def _(c):
            for h in range(2):
                arrive(up_arrivals(c, h, stage - 1))
                start(up_copies(c, h, stage))

    def hand_over(c):
        for h in range(2):
            arrive(up_arrivals(c, h, stages - 2))
            start(up_copies(c, h, stages - 1))

    def iso_stage(stage):
        for step in range(outers):
            o = lax.rem(my_outer + step, outers)
            if stage:
                arrive(iso_arrivals(o, step % 2, stage - 1))
            elif step:
                outer_arrival(step).wait_recv()
            if stage < stages:
                start(iso_copies(o, step % 2, stage))

    for at in range(len(peers)):
        thin_arrival(at).wait_recv()
    hand_over(0)

    @pl.loop(0, bonds * outers)
    def _(q):
        for i in range(per_block):
            isof[pl.ds((q * per_block + i) * own, own), :] = thin[q, i].astype(jnp.float32)

    @pl.loop(0, own)
    def _(k):
        left[pl.ds(k * width, width), :] = isof[pl.ds(k, width, stride=own), :].T.astype(jnp.bfloat16)

    pace = max(1, (chunks - 1) // stages)

    @pl.loop(0, chunks)
    def _(c):
        @pl.when(c + 1 < chunks)
        def _():
            hand_over(c + 1)

        for stage in range(stages):
            @pl.when(c == min(chunks - 1, 1 + stage * pace))
            def _():
                iso_stage(stage)

        for h in range(2):
            arrive(up_arrivals(c, h, stages - 1))

        for pair in range(GROUP):
            h, at = divmod(2 * pair, GROUP)
            w = jnp.concatenate([up[c * 2 + h, :, at + rr].reshape(width, width) for rr in range(2)], axis=1)
            j = jnp.dot(left[...], w, preferred_element_type=jnp.float32).astype(jnp.bfloat16)
            for rr in range(2):
                for k in range(own):
                    joined[h, pl.ds((at + rr) * width, width), pl.ds(k * width, width)] = j[
                        k * width:(k + 1) * width, rr * width:(rr + 1) * width
                    ]
        right = jnp.concatenate([low[d] for d in range(lowers)], axis=1)

        @pl.when(c >= 0)
        def _():
            flat = joined[...].reshape(2 * GROUP * width, own * width)
            product = jnp.dot(flat, right, preferred_element_type=jnp.float32).astype(jnp.bfloat16)
            pairs[pl.ds(c * 2, 2)] = product.reshape(2, *pairs.shape[1:])

    iso_stage(stages)
    take = GROUP // per_block

    @pl.loop(0, 2 * chunks)
    def _(g):
        rows = iso[pl.ds(g * take, take)].reshape(GROUP * width, width)
        lhs = jnp.concatenate([
            jnp.concatenate([
                pairs[g, pl.ds(rr * width, width), pl.ds(d * width, width)] for rr in range(GROUP)
            ], axis=1) for d in range(lowers)
        ], axis=0)
        acc[...] += jnp.dot(lhs, rows, preferred_element_type=jnp.float32).reshape(acc.shape)

    def red_copy(step):
        target = lax.rem(me + step, bonds)
        return pltpu.make_async_remote_copy(
            src_ref=acc.at[:, target], dst_ref=reduced.at[step - 1],
            send_sem=red_send.at[step], recv_sem=red_recv.at[step],
            device_id=(target, my_outer), device_id_type=MESH,
        )

    for step in range(1, bonds):
        red_copy(step).start()
    total = acc[:, me]
    for step in range(1, bonds):
        red_copy(step).wait_recv()
        total = total + reduced[step - 1]
    out_ref[...] = total
    for step in range(1, bonds):
        red_copy(step).wait_send()
    for at in range(len(peers)):
        thin_copy(at).wait_send()
    for step in range(1, outers):
        outer_copy(step).wait_send()
    for stage in range(stages):
        for step in range(outers):
            o = lax.rem(my_outer + step, outers)
            for copy in iso_copies(o, step % 2, stage):
                copy.wait_send()

    @pl.loop(0, chunks)
    def _(c):
        for h in range(2):
            for stage in range(stages):
                for copy in up_copies(c, h, stage):
                    copy.wait_send()


def fused(upper, lower, isometry):
    bonds, outers = lax.axis_size("bond"), lax.axis_size("outer")
    width = isometry.shape[1]
    own, lowers = upper.shape[1], lower.shape[2]
    groups = width // GROUP
    up_in = upper.transpose(2, 1, 0).reshape(groups, GROUP, own, width)
    low = lower.transpose(2, 1, 0, 3).reshape(lowers, own * width, width)
    iso_in = isometry.reshape(-1, width, width)
    bf, f32, dma = jnp.bfloat16, jnp.float32, pltpu.SemaphoreType.DMA
    out = pl.pallas_call(
        functools.partial(kernel, bonds, outers),
        out_shape=jax.ShapeDtypeStruct((lowers, own, width), f32),
        in_specs=[pl.BlockSpec(memory_space=pltpu.VMEM)] * 3,
        out_specs=pl.BlockSpec(memory_space=pltpu.VMEM),
        scratch_shapes=[
            pltpu.VMEM((groups, bonds, GROUP, own, width), bf),
            pltpu.VMEM((bonds * outers, *iso_in.shape), bf),
            pltpu.VMEM((bonds * outers, iso_in.shape[0], own, width), bf),
            pltpu.VMEM((width * own, width), f32),
            pltpu.VMEM((own * width, width), bf),
            pltpu.VMEM((2, GROUP * width, own * width), bf),
            pltpu.VMEM((groups, GROUP * width, lowers * width), bf),
            pltpu.VMEM((lowers, bonds, own, width), f32),
            pltpu.VMEM((bonds - 1, lowers, own, width), f32),
            dma((bonds * outers - 1,)),
            dma((bonds * outers,)),
            dma((groups // 2, 2, bonds - 1)),
            dma((groups // 2, 2, bonds)),
            dma((outers, bonds - 1)),
            dma((outers, bonds)),
            dma((outers,)),
            dma((outers,)),
            dma((bonds,)),
            dma((bonds,)),
        ],
        compiler_params=pltpu.CompilerParams(
            collective_id=0, has_side_effects=True, vmem_limit_bytes=60 * 1024 * 1024
        ),
    )(up_in, low, iso_in)
    return out.transpose(1, 0, 2)


def plain(upper, lower, isometry):
    width = isometry.shape[1]
    own = upper.shape[1]
    iso = lax.all_gather(isometry, ("bond", "outer"), axis=0, tiled=True).reshape(width, width, width)
    whole = lax.all_gather(upper, "bond", axis=1, tiled=True)
    mine = lax.dynamic_slice_in_dim(iso, lax.axis_index("bond") * own, own, 1)

    def column(total, item):
        slab, rows = item
        joined = jnp.einsum("ml,lkx->xkm", slab, mine, preferred_element_type=jnp.float32).astype(jnp.bfloat16)
        paired = jnp.einsum("xkm,mkds->xds", joined, lower, preferred_element_type=jnp.float32).astype(jnp.bfloat16)
        return total + jnp.einsum("xds,sy->xdy", paired, rows, preferred_element_type=jnp.float32), None

    start_total = jnp.zeros((width, lower.shape[2], width), jnp.float32)
    total, _ = lax.scan(column, start_total, (whole.transpose(2, 0, 1), iso))
    return lax.psum_scatter(total, "bond", scatter_dimension=0, tiled=True)


def on_device(upper, lower, isometry):
    bonds = lax.axis_size("bond")
    width = isometry.shape[1]
    rows = isometry.shape[0] // width
    fits = (
        upper.shape[1] % 16 == 0 and bonds >= 4 and bonds & (bonds - 1) == 0
        and width % (2 * GROUP) == 0 and rows > 0 and GROUP % rows == 0
    )
    return (fused if fits else plain)(upper, lower, isometry)


def solution(mesh):
    return jax.shard_map(
        on_device,
        mesh=mesh,
        in_specs=(
            P(None, "bond", None),
            P(None, "bond", "outer", None),
            P(("bond", "outer"), None),
        ),
        out_specs=P("bond", "outer", None),
        check_vma=False,
    )
```
